32 devices in a mesh: sp: 8 (over y, x, core), ch: 4 (over z).
Axes of the slice: x: 2, y: 2, z: 4, core: 2. Of those that a mesh axis runs over, the one named last changes fastest.
Arguments:
- features: bfloat16 [64, 64, 2, 2, 14, 128], P(None, ('sp', 'ch')), may hold values from -6 to 6
- pre_act: bfloat16 [128, 32, 14, 128], P(None, ('sp', 'ch')), may hold values from -6 to 6
- cotangent: bfloat16 [128, 32, 14, 128], P(None, ('sp', 'ch')), may hold values from -12 to 12
- weight: bfloat16 [27, 64, 128], replicated, may hold values from -0.15625 to 0.15625
Outputs:
- data_grad: bfloat16 [64, 64, 2, 2, 14, 128], P(None, ('sp', 'ch'))
- weight_grad: float32 [27, 64, 128], replicated
The draws below stay inside these ranges and needn't reach their ends.
All inputs are finite; a program needn't handle non-finite values.
Results may differ from the reference program's by a relative error of at most 0.0025.
Values may be sent and summed in bfloat16 or wider, within the bound.
A program may use at most 64 MiB of HBM per device.

```python
import math
import jax
import jax.numpy as jnp
from jax import lax

C_IN = 64
C_OUT = 128
TAPS = 27
ROWS_OUT = 14
COLS_OUT = 128
DEP_OUT = 32
DEPTH = 64
OUT_VOX = 57344


def levels(rng, dims, split, smallest, top_value):
    factor_of = 1.0
    for position, shards_of in split:
        heights = jax.random.uniform(jax.random.fold_in(jax.random.fold_in(rng, 6), position), (shards_of,), jnp.float32, smallest / len(split), top_value / len(split))
        factor_of = factor_of * jnp.repeat(jnp.exp(heights), dims[position] // shards_of).reshape((-1,) + (1,) * (len(dims) - 1 - position))
    return factor_of


def centred(own_key, extent, scale, limit, split=(), kind=jnp.bfloat16):
    gain = levels(own_key, extent, split, -0.22, 0.18) if split else 1.0
    values = jax.random.normal(own_key, extent, jnp.float32) * scale * gain
    return jnp.minimum(jnp.maximum(values, -limit), limit).astype(kind)


def setup_inputs(seed: int = 0) -> dict:
    seeds = jax.random.split(jax.random.key(seed), 5)
    return {
        "features": centred(seeds[0], (C_IN, DEPTH, 2, 2, ROWS_OUT, COLS_OUT), 1.0, 6.0, ((1, 32),)),
        "pre_act": centred(seeds[1], (C_OUT, DEP_OUT, ROWS_OUT, COLS_OUT), 1.0, 6.0, ((1, 32),)),
        "cotangent": centred(seeds[2], (C_OUT, DEP_OUT, ROWS_OUT, COLS_OUT), 2.0, 12.0, ((1, 32),)),
        "weight": centred(seeds[3], (TAPS, C_IN, C_OUT), (TAPS * C_IN) ** -0.5, 0.15625),
    }


def shifted(grad_plane, down, right):
    if down:
        grad_plane = jnp.concatenate([grad_plane[:, 1:], jnp.zeros_like(grad_plane[:, :1])], 1)
    if right:
        grad_plane = jnp.concatenate([grad_plane[..., 1:], jnp.zeros_like(grad_plane[..., :1])], -1)
    return grad_plane

def shift_set(grad_plane):
    result = {}
    for down in (0, 1):
        for right in (0, 1):
            result[down, right] = shifted(grad_plane, down, right).reshape(grad_plane.shape[0], -1)
    return result

def tap_parts(tap_pos):
    return (0 if tap_pos == 1 else 1, 1 if tap_pos == 0 else 0)

def weight_terms(depth_planes, grad_set, depth_taps):
    tap_terms = []
    for depth_tap in depth_taps:
        plane = depth_planes[depth_tap]
        for row_tap in range(3):
            row_par, down = tap_parts(row_tap)
            for col_tap in range(3):
                col_par, right = tap_parts(col_tap)
                tap_rows = plane[:, row_par, col_par].reshape(plane.shape[0], -1)
                tap_terms.append(lax.dot_general(tap_rows, grad_set[down, right], (((1,), (1,)), ((), ())), preferred_element_type=jnp.float32))
    return jnp.stack(tap_terms)

def data_terms(weight, here_set, next_set, out_rows, out_cols):
    chans = weight.shape[1]
    groups = {}
    for depth_tap in range(3):
        depth_par = 0 if depth_tap == 1 else 1
        source = next_set if depth_tap == 0 else here_set
        for row_tap in range(3):
            row_par, down = tap_parts(row_tap)
            for col_tap in range(3):
                col_par, right = tap_parts(col_tap)
                key = (depth_par, row_par, col_par)
                if key not in groups:
                    groups[key] = ([], [])
                groups[key][0].append(weight[depth_tap * 9 + row_tap * 3 + col_tap])
                groups[key][1].append(source[down, right])
    results = {}
    for key, pair in groups.items():
        w_rows = jnp.concatenate(pair[0], 1)
        results[key] = jnp.dot(w_rows, jnp.concatenate(pair[1], 0), preferred_element_type=jnp.float32).reshape(chans, out_rows, out_cols)
    depth_parts = []
    for depth_par in range(2):
        row_parts = []
        for row_par in range(2):
            row_parts.append(jnp.stack([results[depth_par, row_par, 0], results[depth_par, row_par, 1]], 1))
        depth_parts.append(jnp.stack(row_parts, 1))
    return jnp.stack(depth_parts, 1).astype(jnp.bfloat16)

def reference(features, pre_act, cotangent, weight):
    masked = jnp.where(pre_act > 0, cotangent, jnp.zeros_like(cotangent))
    padded_in = jnp.pad(features, ((0, 0), (1, 0), (0, 0), (0, 0), (0, 0), (0, 0)))
    padded_out = jnp.pad(masked, ((0, 0), (0, 1), (0, 0), (0, 0)))

    def step(total, block_id):
        start_in = (block_id * 2).astype(jnp.int32)
        prev_plane = lax.dynamic_slice_in_dim(padded_in, start_in, 1, 1)[:, 0]
        block = lax.dynamic_slice_in_dim(features, start_in, 2, 1)
        here = lax.dynamic_slice_in_dim(masked, block_id.astype(jnp.int32), 1, 1)[:, 0]
        after = lax.dynamic_slice_in_dim(padded_out, (block_id + 1).astype(jnp.int32), 1, 1)[:, 0]
        here_set = shift_set(here)
        next_set = shift_set(after)
        planes = {0: prev_plane, 1: block[:, 0], 2: block[:, 1]}
        total = total + weight_terms(planes, here_set, (0, 1, 2))
        return (total, data_terms(weight, here_set, next_set, ROWS_OUT, COLS_OUT))
    start = jnp.zeros((TAPS, C_IN, C_OUT), jnp.float32)
    raw, pieces = lax.scan(step, start, jnp.arange(DEP_OUT, dtype=jnp.int32))
    data_grad = jnp.moveaxis(pieces, 0, 1).reshape(C_IN, DEPTH, 2, 2, ROWS_OUT, COLS_OUT)
    weight_grad = raw * (1.0 / math.sqrt(OUT_VOX))
    return (data_grad, weight_grad)
```

```python
import functools
import math

import jax
import jax.numpy as jnp
from jax import lax
from jax.experimental import pallas as pl
from jax.experimental.pallas import tpu as pltpu
from jax.sharding import PartitionSpec as P

MESH = pl.DeviceIdType.MESH
LANES = 128
UNIT = 8


def kernel(cfg, pre_hbm, cot_hbm, feat_hbm, w_hbm, dg_hbm, wg_hbm, *scr):
    (pre_v, cot_v, feat_v, w_v, m_nat, h_nat, f32s, m32, mh, mn, feat_a, dg_v, grad, out_v) = scr[:14]
    r1, r2, r3 = scr[14:17]
    in_sem, out_sem, halo_s, halo_r, sA, rA = scr[17:]
    chips, chs, rows, c_in, c_out, scale, chunks, taps_first = cfg
    sp = lax.axis_index("sp")
    ch = lax.axis_index("ch")
    chip = sp // 2
    core = sp % 2
    flat = sp * chs + ch
    last = chips * 2 * chs - 1
    span = rows * LANES

    loads = [
        pltpu.make_async_copy(pre_hbm, pre_v, in_sem.at[0]),
        pltpu.make_async_copy(cot_hbm, cot_v, in_sem.at[1]),
        pltpu.make_async_copy(feat_hbm, feat_v, in_sem.at[2]),
        pltpu.make_async_copy(w_hbm, w_v, in_sem.at[3]),
    ]
    for ld in loads:
        ld.start()

    bar = pltpu.get_barrier_semaphore()
    pl.semaphore_signal(bar, inc=1, device_id=(sp + 1 - 2 * core, ch), device_id_type=MESH)
    for k in range(1, chips):
        pl.semaphore_signal(bar, inc=1, device_id=(((chip + k) % chips) * 2 + core, ch), device_id_type=MESH)
    for k in range(1, chs):
        pl.semaphore_signal(bar, inc=1, device_id=(sp, (ch + k) % chs), device_id_type=MESH)
    prev = jnp.maximum(flat - 1, 0)
    nxt = jnp.minimum(flat + 1, last)

    @pl.when(flat > 0)
    def _():
        pl.semaphore_signal(bar, inc=1, device_id=(prev // chs, prev % chs), device_id_type=MESH)

    @pl.when(flat < last)
    def _():
        pl.semaphore_signal(bar, inc=1, device_id=(nxt // chs, nxt % chs), device_id_type=MESH)

    loads[0].wait()
    loads[1].wait()

    cb = 32

    def mask_step(k, carry):
        s = pl.ds(pl.multiple_of(k * cb, cb), cb)
        p = pre_v[s, 0].astype(jnp.float32)
        c = cot_v[s, 0]
        m_nat[s] = jnp.where(p > 0, c.astype(jnp.float32), 0.0).astype(jnp.bfloat16)
        return carry

    lax.fori_loop(0, c_out // cb, mask_step, 0)
    peers = chips + chs - 1 + jnp.minimum(flat, 1) + jnp.minimum(last - flat, 1)
    pl.semaphore_wait(bar, peers)

    halo = pltpu.make_async_remote_copy(
        src_ref=m_nat, dst_ref=h_nat, send_sem=halo_s, recv_sem=halo_r,
        device_id=(prev // chs, prev % chs), device_id_type=MESH,
    )

    @pl.when(flat > 0)
    def _():
        halo.start()

    lane = lax.broadcasted_iota(jnp.int32, (c_out, LANES), 1)

    def relayout_mask(src, dst):
        dst[:, span:] = jnp.zeros((2 * c_out, LANES), jnp.bfloat16)
        m32[:, :rows, :] = src[...].astype(jnp.float32)
        flat32 = m32.reshape(c_out * 16, LANES)
        for b in range(rows):
            v = flat32[pl.ds(b, c_out, stride=16), :]
            dst[:c_out, b * LANES:(b + 1) * LANES] = v.astype(jnp.bfloat16)
            r = jnp.where(lane == LANES - 1, 0.0, pltpu.roll(v, LANES - 1, 1))
            dst[c_out:, b * LANES:(b + 1) * LANES] = r.astype(jnp.bfloat16)

    relayout_mask(m_nat, mh)
    loads[2].wait()

    def feat_step(q, carry):
        p, t, s = q // 4, (q // 2) % 2, q % 2
        buf = f32s.at[q]
        buf[:, :rows, :] = feat_v[:, p, s, t].astype(jnp.float32)
        flat32 = buf.reshape(c_in * 16, LANES)
        for b in range(rows):
            feat_a[q, :, b * LANES:(b + 1) * LANES] = flat32[
                pl.ds(b, c_in, stride=16), :
            ].astype(jnp.bfloat16)
        return carry

    lax.fori_loop(0, 8, feat_step, 0)

    kd_slot = {1: 0, 2: 1, 0: 2}
    ups = c_in // UNIT

    def unit_of(order):
        if order < taps_first:
            return order * ups
        return chunks[1][0] + (order - taps_first) * ups

    def put(kd, kh, kw, val):
        base = unit_of(kd_slot[kd] * 9 + kh * 3 + kw)
        grad[base:base + ups] = val.reshape(ups, UNIT, c_out)

    def wgrad(kd, p, mm):
        dn = (((1,), (1,)), ((), ()))
        t1 = feat_a[p * 4 + 2:p * 4 + 4].reshape(2 * c_in, span)
        o = lax.dot_general(t1, mm[:, :span], dn, preferred_element_type=jnp.float32)
        put(kd, 1, 2, o[:c_in, :c_out])
        put(kd, 1, 0, o[:c_in, c_out:])
        put(kd, 2, 2, o[c_in:, :c_out])
        put(kd, 2, 0, o[c_in:, c_out:])
        t0 = feat_a[p * 4:p * 4 + 2].reshape(2 * c_in, span)
        o = lax.dot_general(t0, mm[:c_out, :span], dn, preferred_element_type=jnp.float32)
        put(kd, 1, 1, o[:c_in])
        put(kd, 2, 1, o[c_in:])
        o = lax.dot_general(feat_a[p * 4 + 3], mm[:, LANES:], dn, preferred_element_type=jnp.float32)
        put(kd, 0, 2, o[:, :c_out])
        put(kd, 0, 0, o[:, c_out:])
        o = lax.dot_general(feat_a[p * 4 + 1], mm[:c_out, LANES:], dn, preferred_element_type=jnp.float32)
        put(kd, 0, 1, o)

    def tap(kd, kh, kw):
        return w_v[kd * 9 + kh * 3 + kw]

    def pair(kd, kh):
        return jnp.concatenate([tap(kd, kh, 2), tap(kd, kh, 0)], 1)

    def dgrad_terms(kd, mm, col):
        def dot(a, b):
            return jnp.dot(a, b, preferred_element_type=jnp.float32)
        here = pl.ds(col, 2 * LANES)
        down = pl.ds(pl.multiple_of(col + LANES, LANES), 2 * LANES)
        t1 = dot(jnp.concatenate([pair(kd, 1), pair(kd, 2)], 0), mm[:, here])
        t1d = dot(pair(kd, 0), mm[:, down])
        t0 = dot(jnp.concatenate([tap(kd, 1, 1), tap(kd, 2, 1)], 0), mm[:c_out, here])
        t0d = dot(tap(kd, 0, 1), mm[:c_out, down])
        return {
            (0, 0): t0[:c_in], (1, 0): t0[c_in:] + t0d,
            (0, 1): t1[:c_in], (1, 1): t1[c_in:] + t1d,
        }

    def dgrad(p, terms):
        def step(k, carry):
            col = pl.multiple_of(k * 2 * LANES, 2 * LANES)
            total = None
            for kd, mm in terms:
                got = dgrad_terms(kd, mm, col)
                total = got if total is None else {key: total[key] + got[key] for key in got}
            for (s, t), val in total.items():
                flat32 = f32s.at[p * 4 + s * 2 + t].reshape(c_in * 16, LANES)
                for j in range(2):
                    flat32[pl.ds(2 * k + j, c_in, stride=16), :] = val[:, j * LANES:(j + 1) * LANES]
            return carry

        lax.fori_loop(0, rows // 2, step, 0)

        def emit(q, carry):
            dg_v[:, p, q // 2, q % 2] = f32s[p * 4 + q, :, :rows, :].astype(jnp.bfloat16)
            return carry

        lax.fori_loop(0, 4, emit, 0)
        return pltpu.make_async_copy(dg_v.at[:, p], dg_hbm.at[:, p], out_sem.at[p])

    class Reduce:
        def __init__(self, idx, base, u):
            self.i, self.base, self.u = idx, base, u
            self.zu = u * chs
            self.half = self.zu * chips
            self.copies = {}

        def remote(self, stage, k, src, dst, dev):
            sem = stage_base[stage] + k
            return pltpu.make_async_remote_copy(
                src_ref=src, dst_ref=dst, send_sem=sA.at[self.i, sem], recv_sem=rA.at[self.i, sem],
                device_id=dev, device_id_type=MESH)

        def chip_dev(self, k):
            return (((chip + k) % chips) * 2 + core, ch)

        def ch_dev(self, k):
            return (sp, (ch + k) % chs)

        def off(self, a, b, c):
            return self.base + (a * self.half) + b * self.zu + c * self.u

        def start(self, stage):
            cps = []
            other = (sp + 1 - 2 * core, ch)
            if stage == 1:
                cps.append(self.remote(1, 0, grad.at[pl.ds(self.off(1 - core, 0, 0), self.half)], r1.at[self.i, pl.ds(0, self.half)], other))
            elif stage == 2:
                for k in range(1, chips):
                    to = (chip + k) % chips
                    cps.append(self.remote(2, k - 1, grad.at[pl.ds(self.off(core, to, 0), self.zu)], r2.at[self.i, k - 1, pl.ds(0, self.zu)], self.chip_dev(k)))
            elif stage == 3:
                for k in range(1, chs):
                    to = (ch + k) % chs
                    cps.append(self.remote(3, k - 1, grad.at[pl.ds(self.off(core, chip, to), self.u)], r3.at[self.i, k - 1, pl.ds(0, self.u)], self.ch_dev(k)))
            elif stage == 4:
                ref = out_v.at[pl.ds(self.off(core, chip, ch), self.u)]
                for k in range(1, chs):
                    cps.append(self.remote(4, k - 1, ref, ref, self.ch_dev(k)))
            elif stage == 5:
                ref = out_v.at[pl.ds(self.off(core, chip, 0), self.zu)]
                for k in range(1, chips):
                    cps.append(self.remote(5, k - 1, ref, ref, self.chip_dev(k)))
            else:
                ref = out_v.at[pl.ds(self.off(core, 0, 0), self.half)]
                cps.append(self.remote(6, 0, ref, ref, other))
            for c in cps:
                c.start()
            self.copies[stage] = cps

        def finish(self, stage):
            for c in self.copies[stage]:
                c.wait_send()
                c.wait_recv()
            if stage == 1:
                s = pl.ds(self.off(core, 0, 0), self.half)
                grad[s] = grad[s] + r1[self.i, :self.half]
            elif stage == 2:
                s = pl.ds(self.off(core, chip, 0), self.zu)
                v = grad[s]
                for k in range(chips - 1):
                    v = v + r2[self.i, k, :self.zu]
                grad[s] = v
            elif stage == 3:
                s = pl.ds(self.off(core, chip, ch), self.u)
                v = grad[s]
                for k in range(chs - 1):
                    v = v + r3[self.i, k, :self.u]
                out_v[s] = v * scale

    stage_base = {1: 0, 2: 1, 3: chips, 4: chips + chs - 1, 5: chips + 2 * chs - 2, 6: 2 * chips + 2 * chs - 3}
    red_a = Reduce(0, *chunks[0])
    red_b = Reduce(1, *chunks[1])

    for lo, hi in ((taps_first * ups, chunks[1][0]), (unit_of(27), grad.shape[0])):
        if lo < hi:
            grad[lo:hi] = jnp.zeros((hi - lo, UNIT, LANES), jnp.float32)

    wgrad(1, 0, mh)
    wgrad(2, 1, mh)
    red_a.start(1)
    loads[3].wait()
    out0 = dgrad(0, [(1, mh)])
    out0.start()
    red_a.finish(1)
    red_a.start(2)

    @pl.when(flat > 0)
    def _():
        halo.wait_send()

    @pl.when(flat < last)
    def _():
        halo.wait_recv()

    @pl.when(flat == last)
    def _():
        h_nat[...] = jnp.zeros_like(h_nat)

    relayout_mask(h_nat, mn)
    wgrad(0, 1, mn)
    red_b.start(1)
    red_a.finish(2)
    red_a.start(3)
    out1 = dgrad(1, [(2, mh), (0, mn)])
    out1.start()
    red_b.finish(1)
    red_b.start(2)
    red_a.finish(3)
    red_a.start(4)
    red_b.finish(2)
    red_b.start(3)
    red_a.finish(4)
    red_a.start(5)
    red_b.finish(3)
    red_b.start(4)
    red_a.finish(5)
    red_a.start(6)
    red_b.finish(4)
    red_b.start(5)
    red_a.finish(6)
    red_b.finish(5)
    red_b.start(6)
    red_b.finish(6)
    outs = []
    for k, (order, count, tap0) in enumerate(
        ((0, taps_first, 9), (taps_first, 18 - taps_first, 9 + taps_first), (18, 9, 0))
    ):
        outs.append(
            pltpu.make_async_copy(
                out_v.at[pl.ds(unit_of(order), count * ups)],
                wg_hbm.at[pl.ds(tap0 * ups, count * ups)],
                out_sem.at[2 + k],
            )
        )
        outs[-1].start()
    out0.wait()
    out1.wait()
    for out in outs:
        out.wait()


def on_device(features, pre_act, cotangent, weight):
    c_in, planes_in, _, _, rows, cols = features.shape
    c_out, planes = pre_act.shape[:2]
    taps = weight.shape[0]
    chips = lax.axis_size("sp") // 2
    chs = lax.axis_size("ch")
    devices = chips * 2 * chs
    scale = 1.0 / math.sqrt(devices * planes * rows * cols)
    ups = c_in // UNIT
    total = taps * ups
    taps_first = 16
    u_a = -(-(taps_first * ups) // devices)
    u_b = -(-(total - taps_first * ups) // devices)
    chunks = ((0, u_a), (u_a * devices, u_b))
    units = (u_a + u_b) * devices
    u_max = max(u_a, u_b)
    n_sems = 2 * chips + 2 * chs - 2
    cfg = (chips, chs, rows, c_in, c_out, scale, chunks, taps_first)
    bf, f32 = jnp.bfloat16, jnp.float32
    span = rows * cols
    any_spec = pl.BlockSpec(memory_space=pl.ANY)
    dg, wg = pl.pallas_call(
        functools.partial(kernel, cfg),
        out_shape=(
            jax.ShapeDtypeStruct(features.shape, bf),
            jax.ShapeDtypeStruct((total, UNIT, c_out), f32),
        ),
        in_specs=[any_spec] * 4,
        out_specs=(any_spec, any_spec),
        scratch_shapes=[
            pltpu.VMEM(pre_act.shape, bf),
            pltpu.VMEM(cotangent.shape, bf),
            pltpu.VMEM(features.shape, bf),
            pltpu.VMEM(weight.shape, bf),
            pltpu.VMEM((c_out, rows, cols), bf),
            pltpu.VMEM((c_out, rows, cols), bf),
            pltpu.VMEM((8, c_in, 16, cols), f32),
            pltpu.VMEM((c_out, 16, cols), f32),
            pltpu.VMEM((2 * c_out, span + cols), bf),
            pltpu.VMEM((2 * c_out, span + cols), bf),
            pltpu.VMEM((8, c_in, span), bf),
            pltpu.VMEM(features.shape, bf),
            pltpu.VMEM((units, UNIT, c_out), f32),
            pltpu.VMEM((units, UNIT, c_out), f32),
            pltpu.VMEM((2, u_max * chs * chips, UNIT, c_out), f32),
            pltpu.VMEM((2, max(1, chips - 1), u_max * chs, UNIT, c_out), f32),
            pltpu.VMEM((2, max(1, chs - 1), u_max, UNIT, c_out), f32),
            pltpu.SemaphoreType.DMA((4,)),
            pltpu.SemaphoreType.DMA((5,)),
            pltpu.SemaphoreType.DMA,
            pltpu.SemaphoreType.DMA,
            pltpu.SemaphoreType.DMA((2, n_sems)),
            pltpu.SemaphoreType.DMA((2, n_sems)),
        ],
        compiler_params=pltpu.CompilerParams(
            collective_id=0, has_side_effects=True, vmem_limit_bytes=56 * 2**20
        ),
    )(pre_act, cotangent, features, weight)
    return dg, wg.reshape(taps, c_in, c_out)


def solution(mesh):
    return jax.shard_map(
        on_device,
        mesh=mesh,
        in_specs=(
            P(None, ("sp", "ch"), None, None, None, None),
            P(None, ("sp", "ch"), None, None),
            P(None, ("sp", "ch"), None, None),
            P(),
        ),
        out_specs=(P(None, ("sp", "ch"), None, None, None, None), P()),
        check_vma=False,
    )
```

```python
import functools
import math

import jax
import jax.numpy as jnp
from jax import lax
from jax.experimental import pallas as pl
from jax.experimental.pallas import tpu as pltpu
from jax.sharding import PartitionSpec as P

MESH = pl.DeviceIdType.MESH
LANES = 128
UNIT = 8


def kernel(cfg, pre_hbm, cot_hbm, feat_hbm, w_hbm, dg_hbm, wg_hbm, *scr):
    (pre_v, cot_v, feat_v, w_v, m_nat, h_nat, mh, mn, feat_a, wl, wf, ws, dg_v, grad, out_v) = scr[:15]
    r1, r2, r3 = scr[15:18]
    in_sem, out_sem, halo_s, halo_r, sA, rA = scr[18:]
    chips, chs, rows, c_in, c_out, scale, chunks, taps_first = cfg
    sp = lax.axis_index("sp")
    ch = lax.axis_index("ch")
    chip = sp // 2
    core = sp % 2
    flat = sp * chs + ch
    last = chips * 2 * chs - 1
    span = rows * LANES

    loads = [
        pltpu.make_async_copy(pre_hbm.at[0], pre_v, in_sem.at[0]),
        pltpu.make_async_copy(cot_hbm.at[0], cot_v, in_sem.at[1]),
        pltpu.make_async_copy(w_hbm, w_v, in_sem.at[2]),
    ]
    for ld in loads:
        ld.start()

    def load_feat(k, carry):
        p, s, b = k // (2 * rows), (k // rows) % 2, k % rows
        pltpu.make_async_copy(feat_hbm.at[:, p, s, b], feat_v.at[p, s, b], in_sem.at[3]).start()
        return carry

    lax.fori_loop(0, 4 * rows, load_feat, 0)

    bar = pltpu.get_barrier_semaphore()
    pl.semaphore_signal(bar, inc=1, device_id=(sp + 1 - 2 * core, ch), device_id_type=MESH)
    for k in range(1, chips):
        pl.semaphore_signal(bar, inc=1, device_id=(((chip + k) % chips) * 2 + core, ch), device_id_type=MESH)
    for k in range(1, chs):
        pl.semaphore_signal(bar, inc=1, device_id=(sp, (ch + k) % chs), device_id_type=MESH)
    prev = jnp.maximum(flat - 1, 0)
    nxt = jnp.minimum(flat + 1, last)

    @pl.when(flat > 0)
    def _():
        pl.semaphore_signal(bar, inc=1, device_id=(prev // chs, prev % chs), device_id_type=MESH)

    @pl.when(flat < last)
    def _():
        pl.semaphore_signal(bar, inc=1, device_id=(nxt // chs, nxt % chs), device_id_type=MESH)

    loads[0].wait()
    loads[1].wait()

    def mask_step(b, carry):
        p = pre_v[b].astype(jnp.float32)
        m_nat[b] = jnp.where(p > 0, cot_v[b].astype(jnp.float32), 0.0).astype(jnp.bfloat16)
        return carry

    lax.fori_loop(0, rows, mask_step, 0)
    peers = chips + chs - 1 + jnp.minimum(flat, 1) + jnp.minimum(last - flat, 1)
    pl.semaphore_wait(bar, peers)

    halo = pltpu.make_async_remote_copy(
        src_ref=m_nat, dst_ref=h_nat, send_sem=halo_s, recv_sem=halo_r,
        device_id=(prev // chs, prev % chs), device_id_type=MESH,
    )

    @pl.when(flat > 0)
    def _():
        halo.start()

    lane = lax.broadcasted_iota(jnp.int32, (c_out, LANES), 1)

    def spread(src, dst):
        dst[:, span:] = jnp.zeros((2 * c_out, LANES), jnp.bfloat16)
        for b in range(rows):
            v = src[b]
            dst[:c_out, b * LANES:(b + 1) * LANES] = v
            r = jnp.where(lane == LANES - 1, 0.0, pltpu.roll(v.astype(jnp.float32), LANES - 1, 1))
            dst[c_out:, b * LANES:(b + 1) * LANES] = r.astype(jnp.bfloat16)

    spread(m_nat, mh)
    pltpu.make_async_copy(feat_v, feat_v, in_sem.at[3]).wait()
    two = 2 * c_in

    feat_rows = feat_v.reshape(2, 2, rows, two, LANES)

    def feat_step(k, carry):
        p, s = k // 2, k % 2
        at = pl.ds(pl.multiple_of(s * two, two), two)
        for b in range(rows):
            feat_a[p, at, b * LANES:(b + 1) * LANES] = feat_rows[p, s, b]
        return carry

    lax.fori_loop(0, 4, feat_step, 0)

    kd_slot = {1: 0, 2: 1, 0: 2}
    ups = c_in // UNIT

    def unit_of(order):
        if order < taps_first:
            return order * ups
        return chunks[1][0] + (order - taps_first) * ups

    def put(kd, kh, kw, val):
        base = unit_of(kd_slot[kd] * 9 + kh * 3 + kw)
        grad[base:base + ups] = val.reshape(ups, UNIT, c_out)

    def wgrad(kd, p, mm):
        dn = (((1,), (1,)), ((), ()))
        o = lax.dot_general(feat_a[p], mm[:, :span], dn, preferred_element_type=jnp.float32)
        d = lax.dot_general(feat_a[p, two:], mm[:, LANES:], dn, preferred_element_type=jnp.float32)
        for r in range(2):
            ws[r, :2 * two] = o[:, r * c_out:(r + 1) * c_out]
            ws[r, 2 * two:] = d[:, r * c_out:(r + 1) * c_out]
        for kh, part in ((1, 0), (2, 1), (0, 2)):
            for kw, r, t in ((1, 0, 0), (2, 0, 1), (0, 1, 1)):
                put(kd, kh, kw, ws[r, pl.ds(part * two + t, c_in, stride=2), :])

    def weights():
        def step(kd, carry):
            for part, kh in enumerate((1, 2, 0)):
                base = kd * 9 + kh * 3
                wf[0, pl.ds(0, c_in, stride=2), :] = w_v[base + 1].astype(jnp.float32)
                wf[0, pl.ds(1, c_in, stride=2), :] = w_v[base + 2].astype(jnp.float32)
                wf[1, pl.ds(0, c_in, stride=2), :] = jnp.zeros((c_in, c_out), jnp.float32)
                wf[1, pl.ds(1, c_in, stride=2), :] = w_v[base].astype(jnp.float32)
                for r in range(2):
                    wl[kd, part * two:(part + 1) * two, r * c_out:(r + 1) * c_out] = wf[r].astype(jnp.bfloat16)
            return carry

        lax.fori_loop(0, 3, step, 0)

    dg_rows = dg_v.reshape(2, 2, rows, two, LANES)

    def dgrad(p, terms):
        def step(k, carry):
            col = pl.multiple_of(k * 2 * LANES, 2 * LANES)
            here = pl.ds(col, 2 * LANES)
            down = pl.ds(pl.multiple_of(col + LANES, LANES), 2 * LANES)
            top, bot = None, None
            for kd, mm in terms:
                o = jnp.dot(wl[kd, :2 * two], mm[:, here], preferred_element_type=jnp.float32)
                d = jnp.dot(wl[kd, 2 * two:], mm[:, down], preferred_element_type=jnp.float32)
                top = o[:two] if top is None else top + o[:two]
                bot = o[two:] + d if bot is None else bot + (o[two:] + d)
            for s, val in ((0, top), (1, bot)):
                for j in range(2):
                    b = 2 * k + j
                    dg_rows[p, s, b] = val[:, j * LANES:(j + 1) * LANES].astype(jnp.bfloat16)
                    pltpu.make_async_copy(dg_v.at[p, s, b], dg_hbm.at[:, p, s, b], out_sem.at[p]).start()
            return carry

        lax.fori_loop(0, rows // 2, step, 0)

    class Reduce:
        def __init__(self, idx, base, u):
            self.i, self.base, self.u = idx, base, u
            self.zu = u * chs
            self.half = self.zu * chips
            self.copies = {}

        def remote(self, stage, k, src, dst, dev):
            sem = stage_base[stage] + k
            return pltpu.make_async_remote_copy(
                src_ref=src, dst_ref=dst, send_sem=sA.at[self.i, sem], recv_sem=rA.at[self.i, sem],
                device_id=dev, device_id_type=MESH)

        def chip_dev(self, k):
            return (((chip + k) % chips) * 2 + core, ch)

        def ch_dev(self, k):
            return (sp, (ch + k) % chs)

        def off(self, a, b, c):
            return self.base + (a * self.half) + b * self.zu + c * self.u

        def start(self, stage):
            cps = []
            other = (sp + 1 - 2 * core, ch)
            if stage == 1:
                cps.append(self.remote(1, 0, grad.at[pl.ds(self.off(1 - core, 0, 0), self.half)], r1.at[self.i, pl.ds(0, self.half)], other))
            elif stage == 2:
                for k in range(1, chips):
                    to = (chip + k) % chips
                    cps.append(self.remote(2, k - 1, grad.at[pl.ds(self.off(core, to, 0), self.zu)], r2.at[self.i, k - 1, pl.ds(0, self.zu)], self.chip_dev(k)))
            elif stage == 3:
                for k in range(1, chs):
                    to = (ch + k) % chs
                    cps.append(self.remote(3, k - 1, grad.at[pl.ds(self.off(core, chip, to), self.u)], r3.at[self.i, k - 1, pl.ds(0, self.u)], self.ch_dev(k)))
            elif stage == 4:
                ref = out_v.at[pl.ds(self.off(core, chip, ch), self.u)]
                for k in range(1, chs):
                    cps.append(self.remote(4, k - 1, ref, ref, self.ch_dev(k)))
            elif stage == 5:
                ref = out_v.at[pl.ds(self.off(core, chip, 0), self.zu)]
                for k in range(1, chips):
                    cps.append(self.remote(5, k - 1, ref, ref, self.chip_dev(k)))
            else:
                ref = out_v.at[pl.ds(self.off(core, 0, 0), self.half)]
                cps.append(self.remote(6, 0, ref, ref, other))
            for c in cps:
                c.start()
            self.copies[stage] = cps

        def finish(self, stage):
            for c in self.copies[stage]:
                c.wait_send()
                c.wait_recv()
            if stage == 1:
                s = pl.ds(self.off(core, 0, 0), self.half)
                grad[s] = grad[s] + r1[self.i, :self.half]
            elif stage == 2:
                s = pl.ds(self.off(core, chip, 0), self.zu)
                v = grad[s]
                for k in range(chips - 1):
                    v = v + r2[self.i, k, :self.zu]
                grad[s] = v
            elif stage == 3:
                s = pl.ds(self.off(core, chip, ch), self.u)
                v = grad[s]
                for k in range(chs - 1):
                    v = v + r3[self.i, k, :self.u]
                out_v[s] = v * scale

    stage_base = {1: 0, 2: 1, 3: chips, 4: chips + chs - 1, 5: chips + 2 * chs - 2, 6: 2 * chips + 2 * chs - 3}
    red_a = Reduce(0, *chunks[0])
    red_b = Reduce(1, *chunks[1])

    for lo, hi in ((taps_first * ups, chunks[1][0]), (unit_of(27), grad.shape[0])):
        if lo < hi:
            grad[lo:hi] = jnp.zeros((hi - lo, UNIT, LANES), jnp.float32)

    wgrad(1, 0, mh)
    wgrad(2, 1, mh)
    red_a.start(1)
    loads[2].wait()
    weights()
    dgrad(0, [(1, mh)])
    red_a.finish(1)
    red_a.start(2)

    @pl.when(flat > 0)
    def _():
        halo.wait_send()

    @pl.when(flat < last)
    def _():
        halo.wait_recv()

    @pl.when(flat == last)
    def _():
        h_nat[...] = jnp.zeros_like(h_nat)

    spread(h_nat, mn)
    wgrad(0, 1, mn)
    red_b.start(1)
    red_a.finish(2)
    red_a.start(3)
    dgrad(1, [(2, mh), (0, mn)])
    red_b.finish(1)
    red_b.start(2)
    red_a.finish(3)
    red_a.start(4)
    red_b.finish(2)
    red_b.start(3)
    red_a.finish(4)
    red_a.start(5)
    red_b.finish(3)
    red_b.start(4)
    red_a.finish(5)
    red_a.start(6)
    red_b.finish(4)
    red_b.start(5)
    red_a.finish(6)
    red_b.finish(5)
    red_b.start(6)
    red_b.finish(6)
    outs = []
    for k, (order, count, tap0) in enumerate(
        ((0, taps_first, 9), (taps_first, 18 - taps_first, 9 + taps_first), (18, 9, 0))
    ):
        outs.append(
            pltpu.make_async_copy(
                out_v.at[pl.ds(unit_of(order), count * ups)],
                wg_hbm.at[pl.ds(tap0 * ups, count * ups)],
                out_sem.at[2 + k],
            )
        )
        outs[-1].start()
    for p in range(2):
        pltpu.make_async_copy(dg_v.at[p], dg_v.at[p], out_sem.at[p]).wait()
    for out in outs:
        out.wait()


def on_device(features, pre_act, cotangent, weight):
    c_in, planes_in, _, _, rows, cols = features.shape
    c_out, planes = pre_act.shape[:2]
    taps = weight.shape[0]
    chips = lax.axis_size("sp") // 2
    chs = lax.axis_size("ch")
    devices = chips * 2 * chs
    scale = 1.0 / math.sqrt(devices * planes * rows * cols)
    ups = c_in // UNIT
    total = taps * ups
    taps_first = 16
    u_a = -(-(taps_first * ups) // devices)
    u_b = -(-(total - taps_first * ups) // devices)
    chunks = ((0, u_a), (u_a * devices, u_b))
    units = (u_a + u_b) * devices
    u_max = max(u_a, u_b)
    n_sems = 2 * chips + 2 * chs - 2
    cfg = (chips, chs, rows, c_in, c_out, scale, chunks, taps_first)
    bf, f32 = jnp.bfloat16, jnp.float32
    span = rows * cols
    any_spec = pl.BlockSpec(memory_space=pl.ANY)
    dg, wg = pl.pallas_call(
        functools.partial(kernel, cfg),
        out_shape=(
            jax.ShapeDtypeStruct((c_in, planes_in, 2, rows, 2, cols), bf),
            jax.ShapeDtypeStruct((total, UNIT, c_out), f32),
        ),
        in_specs=[any_spec] * 4,
        out_specs=(any_spec, any_spec),
        scratch_shapes=[
            pltpu.VMEM((rows, c_out, cols), bf),
            pltpu.VMEM((rows, c_out, cols), bf),
            pltpu.VMEM((2, 2, rows, c_in, 2, cols), bf),
            pltpu.VMEM(weight.shape, bf),
            pltpu.VMEM((rows, c_out, cols), bf),
            pltpu.VMEM((rows, c_out, cols), bf),
            pltpu.VMEM((2 * c_out, span + cols), bf),
            pltpu.VMEM((2 * c_out, span + cols), bf),
            pltpu.VMEM((2, 4 * c_in, span), bf),
            pltpu.VMEM((3, 6 * c_in, 2 * c_out), bf),
            pltpu.VMEM((2, 2 * c_in, c_out), f32),
            pltpu.VMEM((2, 6 * c_in, c_out), f32),
            pltpu.VMEM((2, 2, rows, c_in, 2, cols), bf),
            pltpu.VMEM((units, UNIT, c_out), f32),
            pltpu.VMEM((units, UNIT, c_out), f32),
            pltpu.VMEM((2, u_max * chs * chips, UNIT, c_out), f32),
            pltpu.VMEM((2, max(1, chips - 1), u_max * chs, UNIT, c_out), f32),
            pltpu.VMEM((2, max(1, chs - 1), u_max, UNIT, c_out), f32),
            pltpu.SemaphoreType.DMA((4,)),
            pltpu.SemaphoreType.DMA((5,)),
            pltpu.SemaphoreType.DMA,
            pltpu.SemaphoreType.DMA,
            pltpu.SemaphoreType.DMA((2, n_sems)),
            pltpu.SemaphoreType.DMA((2, n_sems)),
        ],
        compiler_params=pltpu.CompilerParams(
            collective_id=0, has_side_effects=True, vmem_limit_bytes=56 * 2**20
        ),
    )(
        pre_act.transpose(1, 2, 0, 3),
        cotangent.transpose(1, 2, 0, 3),
        features.transpose(0, 1, 2, 4, 3, 5),
        weight,
    )
    return dg.transpose(0, 1, 2, 4, 3, 5), wg.reshape(taps, c_in, c_out)


def solution(mesh):
    return jax.shard_map(
        on_device,
        mesh=mesh,
        in_specs=(
            P(None, ("sp", "ch"), None, None, None, None),
            P(None, ("sp", "ch"), None, None),
            P(None, ("sp", "ch"), None, None),
            P(),
        ),
        out_specs=(P(None, ("sp", "ch"), None, None, None, None), P()),
        check_vma=False,
    )
```

```python
import functools
import math

import jax
import jax.numpy as jnp
from jax import lax
from jax.experimental import pallas as pl
from jax.experimental.pallas import tpu as pltpu
from jax.sharding import PartitionSpec as P

MESH = pl.DeviceIdType.MESH
LANES = 128
UNIT = 8


def kernel(cfg, pre_hbm, cot_hbm, feat_hbm, w_hbm, dg_hbm, wg_hbm, *scr):
    (pre_v, cot_v, feat_v, w_v, m_nat, h_nat, mh, mn, feat_a, wl, wf, ws, dg_v, grad, out_v) = scr[:15]
    r1, r2, r3 = scr[15:18]
    in_sem, out_sem, halo_s, halo_r, sA, rA = scr[18:]
    chips, chs, rows, c_in, c_out, scale, chunks, taps_first = cfg
    sp = lax.axis_index("sp")
    ch = lax.axis_index("ch")
    chip = sp // 2
    core = sp % 2
    flat = sp * chs + ch
    last = chips * 2 * chs - 1
    span = rows * LANES

    loads = [
        pltpu.make_async_copy(pre_hbm.at[0], pre_v, in_sem.at[0]),
        pltpu.make_async_copy(cot_hbm.at[0], cot_v, in_sem.at[1]),
        pltpu.make_async_copy(w_hbm, w_v, in_sem.at[2]),
    ]
    for ld in loads:
        ld.start()

    def load_feat(k, carry):
        p, s, b = k // (2 * rows), (k // rows) % 2, k % rows
        pltpu.make_async_copy(feat_hbm.at[:, p, s, b], feat_v.at[p, s, b], in_sem.at[3]).start()
        return carry

    lax.fori_loop(0, 4 * rows, load_feat, 0)

    bar = pltpu.get_barrier_semaphore()
    pl.semaphore_signal(bar, inc=1, device_id=(sp + 1 - 2 * core, ch), device_id_type=MESH)
    for k in range(1, chips):
        pl.semaphore_signal(bar, inc=1, device_id=(((chip + k) % chips) * 2 + core, ch), device_id_type=MESH)
    for k in range(1, chs):
        pl.semaphore_signal(bar, inc=1, device_id=(sp, (ch + k) % chs), device_id_type=MESH)
    prev = jnp.maximum(flat - 1, 0)
    nxt = jnp.minimum(flat + 1, last)

    @pl.when(flat > 0)
    def _():
        pl.semaphore_signal(bar, inc=1, device_id=(prev // chs, prev % chs), device_id_type=MESH)

    @pl.when(flat < last)
    def _():
        pl.semaphore_signal(bar, inc=1, device_id=(nxt // chs, nxt % chs), device_id_type=MESH)

    loads[0].wait()
    loads[1].wait()

    def mask_step(b, carry):
        p = pre_v[b].astype(jnp.float32)
        m_nat[b] = jnp.where(p > 0, cot_v[b].astype(jnp.float32), 0.0).astype(jnp.bfloat16)
        return carry

    lax.fori_loop(0, rows, mask_step, 0)
    peers = chips + chs - 1 + jnp.minimum(flat, 1) + jnp.minimum(last - flat, 1)
    pl.semaphore_wait(bar, peers)

    halo = pltpu.make_async_remote_copy(
        src_ref=m_nat, dst_ref=h_nat, send_sem=halo_s, recv_sem=halo_r,
        device_id=(prev // chs, prev % chs), device_id_type=MESH,
    )

    @pl.when(flat > 0)
    def _():
        halo.start()

    lane = lax.broadcasted_iota(jnp.int32, (c_out, LANES), 1)

    def spread(src, dst):
        dst[:, span:] = jnp.zeros((2 * c_out, LANES), jnp.bfloat16)
        for b in range(rows):
            v = src[b]
            dst[:c_out, b * LANES:(b + 1) * LANES] = v
            r = jnp.where(lane == LANES - 1, 0.0, pltpu.roll(v.astype(jnp.float32), LANES - 1, 1))
            dst[c_out:, b * LANES:(b + 1) * LANES] = r.astype(jnp.bfloat16)

    spread(m_nat, mh)
    pltpu.make_async_copy(feat_v, feat_v, in_sem.at[3]).wait()
    two = 2 * c_in

    feat_rows = feat_v.reshape(2, 2, rows, two, LANES)

    def feat_step(k, carry):
        p, s = k // 2, k % 2
        at = pl.ds(pl.multiple_of(s * two, two), two)
        for b in range(rows):
            feat_a[p, at, b * LANES:(b + 1) * LANES] = feat_rows[p, s, b]
        return carry

    lax.fori_loop(0, 4, feat_step, 0)

    kd_slot = {1: 0, 2: 1, 0: 2}
    ups = c_in // UNIT

    def unit_of(order):
        if order < taps_first:
            return order * ups
        return chunks[1][0] + (order - taps_first) * ups

    def put(kd, kh, kw, val):
        base = unit_of(kd_slot[kd] * 9 + kh * 3 + kw)
        grad[base:base + ups] = val.reshape(ups, UNIT, c_out)

    def wgrad(kd, p, mm):
        dn = (((1,), (1,)), ((), ()))
        o = lax.dot_general(feat_a[p], mm[:, :span], dn, preferred_element_type=jnp.float32)
        d = lax.dot_general(feat_a[p, two:], mm[:, LANES:], dn, preferred_element_type=jnp.float32)
        for r in range(2):
            ws[r, :2 * two] = o[:, r * c_out:(r + 1) * c_out]
            ws[r, 2 * two:] = d[:, r * c_out:(r + 1) * c_out]
        for kh, part in ((1, 0), (2, 1), (0, 2)):
            for kw, r, t in ((1, 0, 0), (2, 0, 1), (0, 1, 1)):
                put(kd, kh, kw, ws[r, pl.ds(part * two + t, c_in, stride=2), :])

    def weights():
        def step(kd, carry):
            for part, kh in enumerate((1, 2, 0)):
                base = kd * 9 + kh * 3
                wf[0, pl.ds(0, c_in, stride=2), :] = w_v[base + 1].astype(jnp.float32)
                wf[0, pl.ds(1, c_in, stride=2), :] = w_v[base + 2].astype(jnp.float32)
                wf[1, pl.ds(0, c_in, stride=2), :] = jnp.zeros((c_in, c_out), jnp.float32)
                wf[1, pl.ds(1, c_in, stride=2), :] = w_v[base].astype(jnp.float32)
                for r in range(2):
                    wl[kd, part * two:(part + 1) * two, r * c_out:(r + 1) * c_out] = wf[r].astype(jnp.bfloat16)
            return carry

        lax.fori_loop(0, 3, step, 0)

    dg_rows = dg_v.reshape(2, 2, rows, two, LANES)

    def dgrad(p, terms):
        def step(k, carry):
            col = pl.multiple_of(k * 2 * LANES, 2 * LANES)
            here = pl.ds(col, 2 * LANES)
            down = pl.ds(pl.multiple_of(col + LANES, LANES), 2 * LANES)
            top, bot = None, None
            for kd, mm in terms:
                o = jnp.dot(wl[kd, :2 * two], mm[:, here], preferred_element_type=jnp.float32)
                d = jnp.dot(wl[kd, 2 * two:], mm[:, down], preferred_element_type=jnp.float32)
                top = o[:two] if top is None else top + o[:two]
                bot = o[two:] + d if bot is None else bot + (o[two:] + d)
            for s, val in ((0, top), (1, bot)):
                for j in range(2):
                    b = 2 * k + j
                    dg_rows[p, s, b] = val[:, j * LANES:(j + 1) * LANES].astype(jnp.bfloat16)
                    pltpu.make_async_copy(dg_v.at[p, s, b], dg_hbm.at[p, s, b], out_sem.at[p]).start()
            return carry

        lax.fori_loop(0, rows // 2, step, 0)

    class Reduce:
        def __init__(self, idx, base, u):
            self.i, self.base, self.u = idx, base, u
            self.zu = u * chs
            self.half = self.zu * chips
            self.copies = {}

        def remote(self, stage, k, src, dst, dev):
            sem = stage_base[stage] + k
            return pltpu.make_async_remote_copy(
                src_ref=src, dst_ref=dst, send_sem=sA.at[self.i, sem], recv_sem=rA.at[self.i, sem],
                device_id=dev, device_id_type=MESH)

        def chip_dev(self, k):
            return (((chip + k) % chips) * 2 + core, ch)

        def ch_dev(self, k):
            return (sp, (ch + k) % chs)

        def off(self, a, b, c):
            return self.base + (a * self.half) + b * self.zu + c * self.u

        def start(self, stage):
            cps = []
            other = (sp + 1 - 2 * core, ch)
            if stage == 1:
                cps.append(self.remote(1, 0, grad.at[pl.ds(self.off(1 - core, 0, 0), self.half)], r1.at[self.i, pl.ds(0, self.half)], other))
            elif stage == 2:
                for k in range(1, chips):
                    to = (chip + k) % chips
                    cps.append(self.remote(2, k - 1, grad.at[pl.ds(self.off(core, to, 0), self.zu)], r2.at[self.i, k - 1, pl.ds(0, self.zu)], self.chip_dev(k)))
            elif stage == 3:
                for k in range(1, chs):
                    to = (ch + k) % chs
                    cps.append(self.remote(3, k - 1, grad.at[pl.ds(self.off(core, chip, to), self.u)], r3.at[self.i, k - 1, pl.ds(0, self.u)], self.ch_dev(k)))
            elif stage == 4:
                ref = out_v.at[pl.ds(self.off(core, chip, ch), self.u)]
                for k in range(1, chs):
                    cps.append(self.remote(4, k - 1, ref, ref, self.ch_dev(k)))
            elif stage == 5:
                ref = out_v.at[pl.ds(self.off(core, chip, 0), self.zu)]
                for k in range(1, chips):
                    cps.append(self.remote(5, k - 1, ref, ref, self.chip_dev(k)))
            else:
                ref = out_v.at[pl.ds(self.off(core, 0, 0), self.half)]
                cps.append(self.remote(6, 0, ref, ref, other))
            for c in cps:
                c.start()
            self.copies[stage] = cps

        def finish(self, stage):
            for c in self.copies[stage]:
                c.wait_send()
                c.wait_recv()
            if stage == 1:
                s = pl.ds(self.off(core, 0, 0), self.half)
                grad[s] = grad[s] + r1[self.i, :self.half]
            elif stage == 2:
                s = pl.ds(self.off(core, chip, 0), self.zu)
                v = grad[s]
                for k in range(chips - 1):
                    v = v + r2[self.i, k, :self.zu]
                grad[s] = v
            elif stage == 3:
                s = pl.ds(self.off(core, chip, ch), self.u)
                v = grad[s]
                for k in range(chs - 1):
                    v = v + r3[self.i, k, :self.u]
                out_v[s] = v * scale

    stage_base = {1: 0, 2: 1, 3: chips, 4: chips + chs - 1, 5: chips + 2 * chs - 2, 6: 2 * chips + 2 * chs - 3}
    red_a = Reduce(0, *chunks[0])
    red_b = Reduce(1, *chunks[1])

    for lo, hi in ((taps_first * ups, chunks[1][0]), (unit_of(27), grad.shape[0])):
        if lo < hi:
            grad[lo:hi] = jnp.zeros((hi - lo, UNIT, LANES), jnp.float32)

    wgrad(1, 0, mh)
    wgrad(2, 1, mh)
    red_a.start(1)
    loads[2].wait()
    weights()
    red_a.finish(1)
    red_a.start(2)
    dgrad(0, [(1, mh)])
    red_a.finish(2)
    red_a.start(3)

    @pl.when(flat > 0)
    def _():
        halo.wait_send()

    @pl.when(flat < last)
    def _():
        halo.wait_recv()

    @pl.when(flat == last)
    def _():
        h_nat[...] = jnp.zeros_like(h_nat)

    spread(h_nat, mn)
    red_a.finish(3)
    red_a.start(4)
    wgrad(0, 1, mn)
    red_b.start(1)
    red_a.finish(4)
    red_a.start(5)
    red_b.finish(1)
    red_b.start(2)
    dgrad(1, [(2, mh), (0, mn)])
    red_b.finish(2)
    red_b.start(3)
    red_a.finish(5)
    red_a.start(6)
    red_b.finish(3)
    red_b.start(4)
    red_a.finish(6)
    red_b.finish(4)
    red_b.start(5)
    red_b.finish(5)
    red_b.start(6)
    red_b.finish(6)
    outs = []
    for k, (order, count, tap0) in enumerate(
        ((0, taps_first, 9), (taps_first, 18 - taps_first, 9 + taps_first), (18, 9, 0))
    ):
        outs.append(
            pltpu.make_async_copy(
                out_v.at[pl.ds(unit_of(order), count * ups)],
                wg_hbm.at[pl.ds(tap0 * ups, count * ups)],
                out_sem.at[2 + k],
            )
        )
        outs[-1].start()
    for p in range(2):
        pltpu.make_async_copy(dg_v.at[p], dg_v.at[p], out_sem.at[p]).wait()
    for out in outs:
        out.wait()


def store_kernel(dg_in, wg_in, dg_out, wg_out, sem):
    rows = dg_in.shape[2]
    wg_copy = pltpu.make_async_copy(wg_in, wg_out, sem.at[0])
    wg_copy.start()

    def step(k, carry):
        p, s, b = k // (2 * rows), (k // rows) % 2, k % rows
        pltpu.make_async_copy(dg_in.at[p, s, b], dg_out.at[:, p, s, b], sem.at[1]).start()
        return carry

    lax.fori_loop(0, 4 * rows, step, 0)
    pltpu.make_async_copy(dg_in, dg_in, sem.at[1]).wait()
    wg_copy.wait()


def on_device(features, pre_act, cotangent, weight):
    c_in, planes_in, _, _, rows, cols = features.shape
    c_out, planes = pre_act.shape[:2]
    taps = weight.shape[0]
    chips = lax.axis_size("sp") // 2
    chs = lax.axis_size("ch")
    devices = chips * 2 * chs
    scale = 1.0 / math.sqrt(devices * planes * rows * cols)
    ups = c_in // UNIT
    total = taps * ups
    taps_first = 16
    u_a = -(-(taps_first * ups) // devices)
    u_b = -(-(total - taps_first * ups) // devices)
    chunks = ((0, u_a), (u_a * devices, u_b))
    units = (u_a + u_b) * devices
    u_max = max(u_a, u_b)
    n_sems = 2 * chips + 2 * chs - 2
    cfg = (chips, chs, rows, c_in, c_out, scale, chunks, taps_first)
    bf, f32 = jnp.bfloat16, jnp.float32
    held = 2 * (units + u_max * chs * chips + chips * u_max * chs + chs * u_max)
    vmem = 17 * 2**20 + held * UNIT * c_out * 4
    span = rows * cols
    any_spec = pl.BlockSpec(memory_space=pl.ANY)
    dg, wg = pl.pallas_call(
        functools.partial(kernel, cfg),
        out_shape=(
            jax.ShapeDtypeStruct((2, 2, rows, c_in, 2, cols), bf),
            jax.ShapeDtypeStruct((total, UNIT, c_out), f32),
        ),
        in_specs=[pl.BlockSpec(memory_space=pltpu.HBM)] * 4,
        out_specs=(any_spec, any_spec),
        scratch_shapes=[
            pltpu.VMEM((rows, c_out, cols), bf),
            pltpu.VMEM((rows, c_out, cols), bf),
            pltpu.VMEM((2, 2, rows, c_in, 2, cols), bf),
            pltpu.VMEM(weight.shape, bf),
            pltpu.VMEM((rows, c_out, cols), bf),
            pltpu.VMEM((rows, c_out, cols), bf),
            pltpu.VMEM((2 * c_out, span + cols), bf),
            pltpu.VMEM((2 * c_out, span + cols), bf),
            pltpu.VMEM((2, 4 * c_in, span), bf),
            pltpu.VMEM((3, 6 * c_in, 2 * c_out), bf),
            pltpu.VMEM((2, 2 * c_in, c_out), f32),
            pltpu.VMEM((2, 6 * c_in, c_out), f32),
            pltpu.VMEM((2, 2, rows, c_in, 2, cols), bf),
            pltpu.VMEM((units, UNIT, c_out), f32),
            pltpu.VMEM((units, UNIT, c_out), f32),
            pltpu.VMEM((2, u_max * chs * chips, UNIT, c_out), f32),
            pltpu.VMEM((2, max(1, chips - 1), u_max * chs, UNIT, c_out), f32),
            pltpu.VMEM((2, max(1, chs - 1), u_max, UNIT, c_out), f32),
            pltpu.SemaphoreType.DMA((4,)),
            pltpu.SemaphoreType.DMA((5,)),
            pltpu.SemaphoreType.DMA,
            pltpu.SemaphoreType.DMA,
            pltpu.SemaphoreType.DMA((2, n_sems)),
            pltpu.SemaphoreType.DMA((2, n_sems)),
        ],
        compiler_params=pltpu.CompilerParams(
            collective_id=0, has_side_effects=True, vmem_limit_bytes=vmem
        ),
    )(
        pltpu.with_memory_space_constraint(pre_act.transpose(1, 2, 0, 3), pltpu.HBM),
        pltpu.with_memory_space_constraint(cotangent.transpose(1, 2, 0, 3), pltpu.HBM),
        pltpu.with_memory_space_constraint(features.transpose(0, 1, 2, 4, 3, 5), pltpu.HBM),
        pltpu.with_memory_space_constraint(weight, pltpu.HBM),
    )
    dg, wg = pl.pallas_call(
        store_kernel,
        out_shape=(
            jax.ShapeDtypeStruct((c_in, planes_in, 2, rows, 2, cols), bf),
            jax.ShapeDtypeStruct(wg.shape, f32),
        ),
        in_specs=[any_spec] * 2,
        out_specs=(pl.BlockSpec(memory_space=pltpu.HBM),) * 2,
        scratch_shapes=[pltpu.SemaphoreType.DMA((2,))],
        compiler_params=pltpu.CompilerParams(vmem_limit_bytes=2**20),
    )(dg, wg)
    return dg.transpose(0, 1, 2, 4, 3, 5), wg.reshape(taps, c_in, c_out)


def solution(mesh):
    return jax.shard_map(
        on_device,
        mesh=mesh,
        in_specs=(
            P(None, ("sp", "ch"), None, None, None, None),
            P(None, ("sp", "ch"), None, None),
            P(None, ("sp", "ch"), None, None),
            P(),
        ),
        out_specs=(P(None, ("sp", "ch"), None, None, None, None), P()),
        check_vma=False,
    )
```

```python
import functools
import math

import jax
import jax.numpy as jnp
from jax import lax
from jax.experimental import pallas as pl
from jax.experimental.pallas import tpu as pltpu
from jax.sharding import PartitionSpec as P

MESH = pl.DeviceIdType.MESH
LANES = 128
UNIT = 8


def kernel(cfg, pre_hbm, cot_hbm, feat_hbm, w_hbm, dg_hbm, wg_hbm, *scr):
    (pre_v, cot_v, feat_v, w_v, m_nat, h_nat, mh, mn, feat_a, wl, wf, ws, dg_v, grad, out_v) = scr[:15]
    r1, r2, r3 = scr[15:18]
    in_sem, out_sem, halo_s, halo_r, sA, rA = scr[18:]
    chips, chs, rows, c_in, c_out, scale, chunks, taps_first = cfg
    sp = lax.axis_index("sp")
    ch = lax.axis_index("ch")
    chip = sp // 2
    core = sp % 2
    flat = sp * chs + ch
    last = chips * 2 * chs - 1
    span = rows * LANES

    loads = [
        pltpu.make_async_copy(pre_hbm.at[0], pre_v, in_sem.at[0]),
        pltpu.make_async_copy(cot_hbm.at[0], cot_v, in_sem.at[1]),
        pltpu.make_async_copy(w_hbm, w_v, in_sem.at[2]),
    ]
    for ld in loads:
        ld.start()

    def load_feat(k, carry):
        p, s, b = k // (2 * rows), (k // rows) % 2, k % rows
        pltpu.make_async_copy(feat_hbm.at[:, p, s, b], feat_v.at[p, s, b], in_sem.at[3]).start()
        return carry

    lax.fori_loop(0, 4 * rows, load_feat, 0)

    bar = pltpu.get_barrier_semaphore()
    pl.semaphore_signal(bar, inc=1, device_id=(sp + 1 - 2 * core, ch), device_id_type=MESH)
    for k in range(1, chips):
        pl.semaphore_signal(bar, inc=1, device_id=(((chip + k) % chips) * 2 + core, ch), device_id_type=MESH)
    for k in range(1, chs):
        pl.semaphore_signal(bar, inc=1, device_id=(sp, (ch + k) % chs), device_id_type=MESH)
    prev = jnp.maximum(flat - 1, 0)
    nxt = jnp.minimum(flat + 1, last)

    @pl.when(flat > 0)
    def _():
        pl.semaphore_signal(bar, inc=1, device_id=(prev // chs, prev % chs), device_id_type=MESH)

    @pl.when(flat < last)
    def _():
        pl.semaphore_signal(bar, inc=1, device_id=(nxt // chs, nxt % chs), device_id_type=MESH)

    loads[0].wait()
    loads[1].wait()

    def mask_step(b, carry):
        p = pre_v[b].astype(jnp.float32)
        m_nat[b] = jnp.where(p > 0, cot_v[b].astype(jnp.float32), 0.0).astype(jnp.bfloat16)
        return carry

    lax.fori_loop(0, rows, mask_step, 0)
    peers = chips + chs - 1 + jnp.minimum(flat, 1) + jnp.minimum(last - flat, 1)
    pl.semaphore_wait(bar, peers)

    halo = pltpu.make_async_remote_copy(
        src_ref=m_nat, dst_ref=h_nat, send_sem=halo_s, recv_sem=halo_r,
        device_id=(prev // chs, prev % chs), device_id_type=MESH,
    )

    @pl.when(flat > 0)
    def _():
        halo.start()

    lane = lax.broadcasted_iota(jnp.int32, (c_out, LANES), 1)

    def spread(src, dst):
        dst[:, span:] = jnp.zeros((2 * c_out, LANES), jnp.bfloat16)
        for b in range(rows):
            v = src[b]
            dst[:c_out, b * LANES:(b + 1) * LANES] = v
            r = jnp.where(lane == LANES - 1, 0.0, pltpu.roll(v.astype(jnp.float32), LANES - 1, 1))
            dst[c_out:, b * LANES:(b + 1) * LANES] = r.astype(jnp.bfloat16)

    spread(m_nat, mh)
    pltpu.make_async_copy(feat_v, feat_v, in_sem.at[3]).wait()
    two = 2 * c_in

    feat_rows = feat_v.reshape(2, 2, rows, two, LANES)

    def feat_step(k, carry):
        p, s = k // 2, k % 2
        at = pl.ds(pl.multiple_of(s * two, two), two)
        for b in range(rows):
            feat_a[p, at, b * LANES:(b + 1) * LANES] = feat_rows[p, s, b]
        return carry

    lax.fori_loop(0, 4, feat_step, 0)

    kd_slot = {1: 0, 2: 1, 0: 2}
    ups = c_in // UNIT

    def unit_of(order):
        if order < taps_first:
            return order * ups
        return chunks[1][0] + (order - taps_first) * ups

    def put(kd, kh, kw, val):
        base = unit_of(kd_slot[kd] * 9 + kh * 3 + kw)
        grad[base:base + ups] = val.reshape(ups, UNIT, c_out)

    def wgrad(kd, p, mm):
        dn = (((1,), (1,)), ((), ()))
        o = lax.dot_general(feat_a[p], mm[:, :span], dn, preferred_element_type=jnp.float32)
        d = lax.dot_general(feat_a[p, two:], mm[:, LANES:], dn, preferred_element_type=jnp.float32)
        for r in range(2):
            ws[r, :2 * two] = o[:, r * c_out:(r + 1) * c_out]
            ws[r, 2 * two:] = d[:, r * c_out:(r + 1) * c_out]
        for kh, part in ((1, 0), (2, 1), (0, 2)):
            for kw, r, t in ((1, 0, 0), (2, 0, 1), (0, 1, 1)):
                put(kd, kh, kw, ws[r, pl.ds(part * two + t, c_in, stride=2), :])

    def weights():
        def step(kd, carry):
            for part, kh in enumerate((1, 2, 0)):
                base = kd * 9 + kh * 3
                wf[0, pl.ds(0, c_in, stride=2), :] = w_v[base + 1].astype(jnp.float32)
                wf[0, pl.ds(1, c_in, stride=2), :] = w_v[base + 2].astype(jnp.float32)
                wf[1, pl.ds(0, c_in, stride=2), :] = jnp.zeros((c_in, c_out), jnp.float32)
                wf[1, pl.ds(1, c_in, stride=2), :] = w_v[base].astype(jnp.float32)
                for r in range(2):
                    wl[kd, part * two:(part + 1) * two, r * c_out:(r + 1) * c_out] = wf[r].astype(jnp.bfloat16)
            return carry

        lax.fori_loop(0, 3, step, 0)

    dg_rows = dg_v.reshape(2, 2, rows, two, LANES)

    def dgrad(p, terms):
        def step(k, carry):
            col = pl.multiple_of(k * 2 * LANES, 2 * LANES)
            here = pl.ds(col, 2 * LANES)
            down = pl.ds(pl.multiple_of(col + LANES, LANES), 2 * LANES)
            top, bot = None, None
            for kd, mm in terms:
                o = jnp.dot(wl[kd, :2 * two], mm[:, here], preferred_element_type=jnp.float32)
                d = jnp.dot(wl[kd, 2 * two:], mm[:, down], preferred_element_type=jnp.float32)
                top = o[:two] if top is None else top + o[:two]
                bot = o[two:] + d if bot is None else bot + (o[two:] + d)
            for s, val in ((0, top), (1, bot)):
                for j in range(2):
                    b = 2 * k + j
                    dg_rows[p, s, b] = val[:, j * LANES:(j + 1) * LANES].astype(jnp.bfloat16)
                    pltpu.make_async_copy(dg_v.at[p, s, b], dg_hbm.at[p, s, b], out_sem.at[p]).start()
            return carry

        lax.fori_loop(0, rows // 2, step, 0)

    class Reduce:
        def __init__(self, idx, base, u):
            self.i, self.base, self.u = idx, base, u
            self.zu = u * chs
            self.half = self.zu * chips
            self.copies = {}

        def remote(self, stage, k, src, dst, dev):
            sem = stage_base[stage] + k
            return pltpu.make_async_remote_copy(
                src_ref=src, dst_ref=dst, send_sem=sA.at[self.i, sem], recv_sem=rA.at[self.i, sem],
                device_id=dev, device_id_type=MESH)

        def chip_dev(self, k):
            return (((chip + k) % chips) * 2 + core, ch)

        def ch_dev(self, k):
            return (sp, (ch + k) % chs)

        def off(self, a, b, c):
            return self.base + (a * self.half) + b * self.zu + c * self.u

        def start(self, stage):
            cps = []
            other = (sp + 1 - 2 * core, ch)
            if stage == 1:
                cps.append(self.remote(1, 0, grad.at[pl.ds(self.off(1 - core, 0, 0), self.half)], r1.at[self.i, pl.ds(0, self.half)], other))
            elif stage == 2:
                for k in range(1, chips):
                    to = (chip + k) % chips
                    cps.append(self.remote(2, k - 1, grad.at[pl.ds(self.off(core, to, 0), self.zu)], r2.at[self.i, k - 1, pl.ds(0, self.zu)], self.chip_dev(k)))
            elif stage == 3:
                for k in range(1, chs):
                    to = (ch + k) % chs
                    cps.append(self.remote(3, k - 1, grad.at[pl.ds(self.off(core, chip, to), self.u)], r3.at[self.i, k - 1, pl.ds(0, self.u)], self.ch_dev(k)))
            elif stage == 4:
                ref = out_v.at[pl.ds(self.off(core, chip, ch), self.u)]
                for k in range(1, chs):
                    cps.append(self.remote(4, k - 1, ref, ref, self.ch_dev(k)))
            elif stage == 5:
                ref = out_v.at[pl.ds(self.off(core, chip, 0), self.zu)]
                for k in range(1, chips):
                    cps.append(self.remote(5, k - 1, ref, ref, self.chip_dev(k)))
            else:
                ref = out_v.at[pl.ds(self.off(core, 0, 0), self.half)]
                cps.append(self.remote(6, 0, ref, ref, other))
            for c in cps:
                c.start()
            self.copies[stage] = cps

        def finish(self, stage):
            for c in self.copies[stage]:
                c.wait_send()
                c.wait_recv()
            if stage == 1:
                s = pl.ds(self.off(core, 0, 0), self.half)
                grad[s] = grad[s] + r1[self.i, :self.half]
            elif stage == 2:
                s = pl.ds(self.off(core, chip, 0), self.zu)
                v = grad[s]
                for k in range(chips - 1):
                    v = v + r2[self.i, k, :self.zu]
                grad[s] = v
            elif stage == 3:
                s = pl.ds(self.off(core, chip, ch), self.u)
                v = grad[s]
                for k in range(chs - 1):
                    v = v + r3[self.i, k, :self.u]
                out_v[s] = v * scale

    stage_base = {1: 0, 2: 1, 3: chips, 4: chips + chs - 1, 5: chips + 2 * chs - 2, 6: 2 * chips + 2 * chs - 3}
    red_a = Reduce(0, *chunks[0])
    red_b = Reduce(1, *chunks[1])

    for lo, hi in ((taps_first * ups, chunks[1][0]), (unit_of(27), grad.shape[0])):
        if lo < hi:
            grad[lo:hi] = jnp.zeros((hi - lo, UNIT, LANES), jnp.float32)

    wgrad(1, 0, mh)
    wgrad(2, 1, mh)
    red_a.start(1)
    loads[2].wait()
    weights()
    dgrad(0, [(1, mh)])
    red_a.finish(1)
    red_a.start(2)

    @pl.when(flat > 0)
    def _():
        halo.wait_send()

    @pl.when(flat < last)
    def _():
        halo.wait_recv()

    @pl.when(flat == last)
    def _():
        h_nat[...] = jnp.zeros_like(h_nat)

    spread(h_nat, mn)
    wgrad(0, 1, mn)
    red_b.start(1)
    red_a.finish(2)
    red_a.start(3)
    dgrad(1, [(2, mh), (0, mn)])
    red_b.finish(1)
    red_b.start(2)
    red_a.finish(3)
    red_a.start(4)
    red_b.finish(2)
    red_b.start(3)
    red_a.finish(4)
    red_a.start(5)
    red_b.finish(3)
    red_b.start(4)
    red_a.finish(5)
    red_a.start(6)
    red_b.finish(4)
    red_b.start(5)
    red_a.finish(6)
    red_b.finish(5)
    red_b.start(6)
    red_b.finish(6)
    outs = []
    for k, (order, count, tap0) in enumerate(
        ((0, taps_first, 9), (taps_first, 18 - taps_first, 9 + taps_first), (18, 9, 0))
    ):
        outs.append(
            pltpu.make_async_copy(
                out_v.at[pl.ds(unit_of(order), count * ups)],
                wg_hbm.at[pl.ds(tap0 * ups, count * ups)],
                out_sem.at[2 + k],
            )
        )
        outs[-1].start()
    for p in range(2):
        pltpu.make_async_copy(dg_v.at[p], dg_v.at[p], out_sem.at[p]).wait()
    for out in outs:
        out.wait()


def store_kernel(dg_in, wg_in, dg_out, wg_out, sem):
    rows = dg_in.shape[2]
    wg_copy = pltpu.make_async_copy(wg_in, wg_out, sem.at[0])
    wg_copy.start()

    def step(k, carry):
        p, s, b = k // (2 * rows), (k // rows) % 2, k % rows
        pltpu.make_async_copy(dg_in.at[p, s, b], dg_out.at[:, p, s, b], sem.at[1]).start()
        return carry

    lax.fori_loop(0, 4 * rows, step, 0)
    pltpu.make_async_copy(dg_in, dg_in, sem.at[1]).wait()
    wg_copy.wait()


def on_device(features, pre_act, cotangent, weight):
    c_in, planes_in, _, _, rows, cols = features.shape
    c_out, planes = pre_act.shape[:2]
    taps = weight.shape[0]
    chips = lax.axis_size("sp") // 2
    chs = lax.axis_size("ch")
    devices = chips * 2 * chs
    scale = 1.0 / math.sqrt(devices * planes * rows * cols)
    ups = c_in // UNIT
    total = taps * ups
    taps_first = 16
    u_a = -(-(taps_first * ups) // devices)
    u_b = -(-(total - taps_first * ups) // devices)
    chunks = ((0, u_a), (u_a * devices, u_b))
    units = (u_a + u_b) * devices
    u_max = max(u_a, u_b)
    n_sems = 2 * chips + 2 * chs - 2
    cfg = (chips, chs, rows, c_in, c_out, scale, chunks, taps_first)
    bf, f32 = jnp.bfloat16, jnp.float32
    held = 2 * (units + u_max * chs * chips + chips * u_max * chs + chs * u_max)
    vmem = 17 * 2**20 + held * UNIT * c_out * 4
    span = rows * cols
    any_spec = pl.BlockSpec(memory_space=pl.ANY)
    dg, wg = pl.pallas_call(
        functools.partial(kernel, cfg),
        out_shape=(
            jax.ShapeDtypeStruct((2, 2, rows, c_in, 2, cols), bf),
            jax.ShapeDtypeStruct((total, UNIT, c_out), f32),
        ),
        in_specs=[pl.BlockSpec(memory_space=pltpu.HBM)] * 4,
        out_specs=(any_spec, any_spec),
        scratch_shapes=[
            pltpu.VMEM((rows, c_out, cols), bf),
            pltpu.VMEM((rows, c_out, cols), bf),
            pltpu.VMEM((2, 2, rows, c_in, 2, cols), bf),
            pltpu.VMEM(weight.shape, bf),
            pltpu.VMEM((rows, c_out, cols), bf),
            pltpu.VMEM((rows, c_out, cols), bf),
            pltpu.VMEM((2 * c_out, span + cols), bf),
            pltpu.VMEM((2 * c_out, span + cols), bf),
            pltpu.VMEM((2, 4 * c_in, span), bf),
            pltpu.VMEM((3, 6 * c_in, 2 * c_out), bf),
            pltpu.VMEM((2, 2 * c_in, c_out), f32),
            pltpu.VMEM((2, 6 * c_in, c_out), f32),
            pltpu.VMEM((2, 2, rows, c_in, 2, cols), bf),
            pltpu.VMEM((units, UNIT, c_out), f32),
            pltpu.VMEM((units, UNIT, c_out), f32),
            pltpu.VMEM((2, u_max * chs * chips, UNIT, c_out), f32),
            pltpu.VMEM((2, max(1, chips - 1), u_max * chs, UNIT, c_out), f32),
            pltpu.VMEM((2, max(1, chs - 1), u_max, UNIT, c_out), f32),
            pltpu.SemaphoreType.DMA((4,)),
            pltpu.SemaphoreType.DMA((5,)),
            pltpu.SemaphoreType.DMA,
            pltpu.SemaphoreType.DMA,
            pltpu.SemaphoreType.DMA((2, n_sems)),
            pltpu.SemaphoreType.DMA((2, n_sems)),
        ],
        compiler_params=pltpu.CompilerParams(
            collective_id=0, has_side_effects=True, vmem_limit_bytes=vmem
        ),
    )(
        pltpu.with_memory_space_constraint(pre_act.transpose(1, 2, 0, 3), pltpu.HBM),
        pltpu.with_memory_space_constraint(cotangent.transpose(1, 2, 0, 3), pltpu.HBM),
        pltpu.with_memory_space_constraint(features.transpose(0, 1, 2, 4, 3, 5), pltpu.HBM),
        pltpu.with_memory_space_constraint(weight, pltpu.HBM),
    )
    dg, wg = pl.pallas_call(
        store_kernel,
        out_shape=(
            jax.ShapeDtypeStruct((c_in, planes_in, 2, rows, 2, cols), bf),
            jax.ShapeDtypeStruct(wg.shape, f32),
        ),
        in_specs=[any_spec] * 2,
        out_specs=(pl.BlockSpec(memory_space=pltpu.HBM),) * 2,
        scratch_shapes=[pltpu.SemaphoreType.DMA((2,))],
        compiler_params=pltpu.CompilerParams(vmem_limit_bytes=2**20),
    )(dg, wg)
    return dg.transpose(0, 1, 2, 4, 3, 5), wg.reshape(taps, c_in, c_out)


def solution(mesh):
    return jax.shard_map(
        on_device,
        mesh=mesh,
        in_specs=(
            P(None, ("sp", "ch"), None, None, None, None),
            P(None, ("sp", "ch"), None, None),
            P(None, ("sp", "ch"), None, None),
            P(),
        ),
        out_specs=(P(None, ("sp", "ch"), None, None, None, None), P()),
        check_vma=False,
    )
```
